32 devices in a mesh: hid: 8 (over z, y), dp: 4 (over x, core).
Axes of the slice: x: 2, y: 2, z: 4, core: 2. Of those that a mesh axis runs over, the one named last changes fastest.
Arguments:
- hidden_acts: bfloat16 [1024, 65536], P('dp', 'hid'), may hold values from -6 to 6
- out_grads: bfloat16 [1024, 1024], P('dp'), may hold values from -6 to 6
- damping: float32 [64], replicated, may hold values from 0.05 to 1
Outputs:
- update: bfloat16 [65536, 1024], P('hid')
The draws below stay inside these ranges and needn't reach their ends.
All inputs are finite; a program needn't handle non-finite values.
Results may differ from the reference program's by a relative error of at most 0.0023.
Values may be sent and summed in bfloat16 or wider, within the bound.
No kernel may reach another device: no remote copies, remote signals or barrier semaphores. Data moves between devices by JAX's collectives and lax.ppermute only.
A program may use at most 128 MiB of HBM per device.

```python
import math
import jax
import jax.numpy as jnp
from jax import lax

D = 1024
FF = 65536
BLOCK = 1024
ITERS = 3
TOKENS = 1024
BLOCKS = 64


def level_of(own_key, shape, pieces, least, top_value):
    def one(position, blocks):
        heights = jax.random.uniform(jax.random.fold_in(jax.random.fold_in(own_key, 6), position), (blocks,), jnp.float32, least / len(pieces), top_value / len(pieces))
        return jnp.repeat(jnp.exp(heights), shape[position] // blocks).reshape((-1,) + (1,) * (len(shape) - position - 1))

    level = one(*pieces[0])
    for cut in pieces[1:]:
        level = level * one(*cut)
    return level


def centred(stream_key, extent, width, limit, pieces=(), held_as=jnp.bfloat16):
    array = width * jax.random.normal(stream_key, extent, jnp.float32)
    if pieces:
        array = array * level_of(stream_key, extent, pieces, -0.22, 0.18)
    return jnp.clip(array, -limit, limit).astype(held_as)


def setup_inputs(seed: int = 0) -> dict:
    seeds = jax.random.split(jax.random.key(seed), 4)
    hidden_acts = centred(seeds[0], (TOKENS, FF), 1.0, 6.0, ((0, 4), (1, 8)))
    out_grads = centred(seeds[1], (TOKENS, D), 1.0, 6.0, ((0, 4),))
    damping = jnp.clip(jnp.exp(jax.random.uniform(seeds[2], (BLOCKS,), jnp.float32, math.log(0.05), math.log(1.0))), 0.05, 1.0)
    return {"hidden_acts": hidden_acts, "out_grads": out_grads, "damping": damping}


out_damping = 0.1

def newton(matrix):
    order = matrix.shape[0]
    start_scale = 1.0 / jnp.sqrt(jnp.sum(matrix * matrix))
    inverse = start_scale * jnp.eye(order, dtype=jnp.float32)
    for iteration in range(ITERS):
        product = jnp.dot(matrix, inverse, precision=lax.Precision.HIGHEST)
        product = jnp.dot(product, inverse, precision=lax.Precision.HIGHEST)
        inverse = 2.0 * inverse - product
    return inverse

def reference(hidden_acts, out_grads, damping):
    out_factor = jnp.dot(out_grads.T, out_grads, preferred_element_type=jnp.float32) / TOKENS
    out_factor = out_factor + out_damping * jnp.eye(D, dtype=jnp.float32)
    out_inverse = newton(out_factor)
    hidden_blocks = hidden_acts.reshape(TOKENS, BLOCKS, BLOCK).transpose(1, 0, 2)

    def per_block(inputs):
        columns, block_damping = inputs
        in_factor = jnp.dot(columns.T, columns, preferred_element_type=jnp.float32) / TOKENS
        in_factor = in_factor + block_damping * jnp.eye(BLOCK, dtype=jnp.float32)
        in_inverse = newton(in_factor)
        grad = jnp.dot(columns.T, out_grads, preferred_element_type=jnp.float32)
        right = jnp.dot(grad, out_inverse, precision=lax.Precision.HIGHEST)
        return jnp.dot(in_inverse, right, precision=lax.Precision.HIGHEST).astype(jnp.bfloat16)
    result = lax.map(per_block, (hidden_blocks, damping))
    return result.reshape(FF, D)
```

```python
import functools

import jax
import jax.numpy as jnp
from jax import lax
from jax.experimental import pallas as pl
from jax.experimental.pallas import tpu as pltpu
from jax.sharding import PartitionSpec as P


BLOCK = 1024
ITERS = 3
OUT_DAMPING = 0.1
KERNEL_VMEM = 36 * 2**20


ANY = pl.BlockSpec(memory_space=pl.ANY)
VMEM = pl.BlockSpec(memory_space=pltpu.VMEM)
SMEM = pl.BlockSpec(memory_space=pltpu.SMEM)
NN = (((1,), (0,)), ((), ()))
TN = (((0,), (0,)), ((), ()))


def dot(a, b, dims=NN):
    return lax.dot_general(a, b, dims, preferred_element_type=jnp.float32)


def swap(value, mask):
    pairs = [(source, source ^ mask) for source in range(lax.axis_size("dp"))]
    return lax.ppermute(value, "dp", pairs)


def eye_chunk(first, rows, width):
    row_ids = lax.broadcasted_iota(jnp.int32, (rows, width), 0) + first
    return row_ids == lax.broadcasted_iota(jnp.int32, (rows, width), 1)


def scaled_factor(acts, factor, damping, tokens, chunk=256):
    width = acts.shape[1]
    total = jnp.zeros((1, width), jnp.float32)
    for lo in range(0, width, chunk):
        rows = dot(acts[:, lo : lo + chunk], acts[...], TN) * (1.0 / tokens)
        rows = rows + jnp.where(eye_chunk(lo, chunk, width), damping, 0.0)
        factor[lo : lo + chunk, :] = rows
        total = total + jnp.sum(rows * rows, axis=0, keepdims=True)
    return 1.0 / jnp.sqrt(jnp.sum(total, axis=1, keepdims=True))


def residual_powers(factor, scale, powers, chunk=256):
    width = factor.shape[0]
    steps = range(0, width, chunk)
    for lo in steps:
        rows = factor[lo : lo + chunk, :] * scale
        factor[lo : lo + chunk, :] = rows
        powers[0, lo : lo + chunk, :] = rows.astype(jnp.bfloat16)

    def square(k, carry):
        for lo in steps:
            rows = slice(lo, lo + chunk)
            value = 2.0 * factor[rows, :] - dot(powers[k, rows, :], powers[k])
            factor[rows, :] = value
            powers[k + 1, rows, :] = value.astype(jnp.bfloat16)
        return carry

    lax.fori_loop(0, ITERS - 1, square, 0)


def out_kernel(parts, tokens, *refs):
    pieces = refs[:parts]
    high_ref, low_ref, grads, factor, powers, wide, narrow, sem = refs[parts:]
    span = pieces[0].shape[0]
    copies = []
    for part in range(parts):
        copy = pltpu.make_async_copy(
            pieces[part], grads.at[pl.ds(part * span, span)], sem.at[part]
        )
        copy.start()
        copies.append(copy)
    for copy in copies:
        copy.wait()
    scale = scaled_factor(grads, factor, OUT_DAMPING, tokens)
    residual_powers(factor, scale, powers)
    chunk = 256
    for lo in range(0, tokens, chunk):
        wide[lo : lo + chunk, :] = grads[lo : lo + chunk, :].astype(jnp.float32) * scale
    narrow[...] = wide[...].astype(jnp.bfloat16)

    def apply(turn, carry):
        for lo in range(0, tokens, chunk):
            rows = slice(lo, lo + chunk)
            value = 2.0 * wide[rows, :] - dot(narrow[rows, :], powers[ITERS - 1 - turn])
            wide[rows, :] = value
            narrow[rows, :] = value.astype(jnp.bfloat16)
        return carry

    lax.fori_loop(0, ITERS, apply, 0)
    for lo in range(0, tokens, chunk):
        rows = slice(lo, lo + chunk)
        high = narrow[rows, :]
        high_ref[rows, :] = high
        low_ref[rows, :] = (wide[rows, :] - high.astype(jnp.float32)).astype(jnp.bfloat16)


def precondition_grads(pieces, tokens):
    _, width = pieces[0].shape
    parts = len(pieces)
    return pl.pallas_call(
        functools.partial(out_kernel, parts, tokens),
        out_shape=[jax.ShapeDtypeStruct((tokens, width), jnp.bfloat16)] * 2,
        in_specs=[VMEM] * parts,
        out_specs=[VMEM] * 2,
        scratch_shapes=[
            pltpu.VMEM((tokens, width), jnp.bfloat16),
            pltpu.VMEM((width, width), jnp.float32),
            pltpu.VMEM((ITERS, width, width), jnp.bfloat16),
            pltpu.VMEM((tokens, width), jnp.float32),
            pltpu.VMEM((tokens, width), jnp.bfloat16),
            pltpu.SemaphoreType.DMA((parts,)),
        ],
        compiler_params=pltpu.CompilerParams(vmem_limit_bytes=KERNEL_VMEM),
        name="out_side",
    )(*pieces)


def place_copy(back_ref, whole_ref, block, sem):
    return pltpu.make_async_copy(
        back_ref, whole_ref.at[pl.ds(pl.multiple_of(block * BLOCK, BLOCK), BLOCK)], sem
    )


def block_kernel(step, parts, tokens, landed, held, *refs):
    damping_ref, acts_ref = refs[:2]
    pieces = refs[2 : 1 + parts]
    refs = refs[1 + parts :]
    spread_refs = refs[:2]
    refs = refs[2:]
    back_ref = None
    if landed:
        back_ref = refs[0]
        refs = refs[1:]
    if held:
        refs = refs[1:]
    whole_ref, send_ref = refs[:2]
    acts, spread, factor, powers, wide, sem = refs[2:]
    core = lax.axis_index("dp") % 2
    span = acts_ref.shape[0]
    blocks = acts_ref.shape[1] // BLOCK
    column = pl.multiple_of((2 * step + core) * BLOCK, BLOCK)
    copies = [
        pltpu.make_async_copy(
            acts_ref.at[:, pl.ds(column, BLOCK)], acts.at[pl.ds(0, span)], sem.at[0]
        )
    ] + [
        pltpu.make_async_copy(piece, acts.at[pl.ds((part + 1) * span, span)], sem.at[part + 1])
        for part, piece in enumerate(pieces)
    ]
    later = [
        pltpu.make_async_copy(spread_refs[half], spread.at[half], sem.at[parts + half])
        for half in range(2)
    ]
    if landed:
        placing = place_copy(back_ref, whole_ref, 2 * (step - 2) + 1 - core, sem.at[parts + 2])
        placing.start()
    for copy in copies + later:
        copy.start()
    for copy in copies:
        copy.wait()
    damping = damping_ref[lax.axis_index("hid") * blocks + 2 * step + core]
    scale = scaled_factor(acts, factor, damping, tokens)
    residual_powers(factor, scale, powers)
    for copy in later:
        copy.wait()
    chunk = 256
    width = send_ref.shape[1]
    wide[...] = jnp.zeros_like(wide)

    def gather(half, carry):
        for lo in range(0, BLOCK, chunk):
            rows = slice(lo, lo + chunk)
            value = wide[rows, :] + dot(acts[:, rows], spread[half], TN)
            wide[rows, :] = value
        return carry

    lax.fori_loop(0, 2, gather, 0)
    for lo in range(0, BLOCK, chunk):
        rows = slice(lo, lo + chunk)
        value = wide[rows, :] * scale
        wide[rows, :] = value
        send_ref[rows, :] = value.astype(jnp.bfloat16)

    def apply(turn, carry):
        for lo in range(0, width, chunk):
            cols = slice(lo, lo + chunk)
            value = 2.0 * wide[:, cols] - dot(powers[ITERS - 1 - turn], send_ref[:, cols])
            wide[:, cols] = value
            send_ref[:, cols] = value.astype(jnp.bfloat16)
        return carry

    lax.fori_loop(0, ITERS, apply, 0)
    storing = place_copy(send_ref, whole_ref, 2 * step + core, sem.at[0])
    storing.start()
    if landed:
        placing.wait()
    storing.wait()


def precondition_block(step, tokens, damping, acts, pieces, spread, back, whole):
    parts = len(pieces) + 1
    width = spread[0].shape[1]
    landed, held = back is not None, whole is not None
    operands = [damping, acts, *pieces, *spread]
    specs = [SMEM, ANY] + [VMEM] * len(pieces) + [ANY] * 2
    aliases = {}
    if landed:
        operands.append(back)
        specs.append(VMEM)
    if held:
        operands.append(whole)
        specs.append(ANY)
        aliases = {len(operands) - 1: 0}
    return pl.pallas_call(
        functools.partial(block_kernel, step, parts, tokens, landed, held),
        out_shape=[
            jax.ShapeDtypeStruct((acts.shape[1], width), jnp.bfloat16),
            jax.ShapeDtypeStruct((BLOCK, width), jnp.bfloat16),
        ],
        in_specs=specs,
        out_specs=[ANY, VMEM],
        input_output_aliases=aliases,
        scratch_shapes=[
            pltpu.VMEM((tokens, BLOCK), jnp.bfloat16),
            pltpu.VMEM((2, tokens, width), jnp.bfloat16),
            pltpu.VMEM((BLOCK, BLOCK), jnp.float32),
            pltpu.VMEM((ITERS, BLOCK, BLOCK), jnp.bfloat16),
            pltpu.VMEM((BLOCK, width), jnp.float32),
            pltpu.SemaphoreType.DMA((parts + 3,)),
        ],
        compiler_params=pltpu.CompilerParams(vmem_limit_bytes=KERNEL_VMEM),
        name="block_side",
    )(*operands)


def place_kernel(step, back_ref, held_ref, whole_ref, sem):
    copy = place_copy(back_ref, whole_ref, 2 * step + 1 - lax.axis_index("dp") % 2, sem)
    copy.start()
    copy.wait()


def place(step, back, whole):
    return pl.pallas_call(
        functools.partial(place_kernel, step),
        out_shape=jax.ShapeDtypeStruct(whole.shape, whole.dtype),
        in_specs=[VMEM, ANY],
        out_specs=ANY,
        input_output_aliases={1: 0},
        scratch_shapes=[pltpu.SemaphoreType.DMA(())],
        name="place",
    )(back, whole)


def local(hidden_acts, out_grads, damping):
    dp_size = lax.axis_size("dp")
    tokens = hidden_acts.shape[0] * dp_size
    core = lax.axis_index("dp") % 2
    steps = hidden_acts.shape[1] // BLOCK // 2
    masks = [1 << bit for bit in reversed(range(dp_size.bit_length() - 1))]

    grads = {0: out_grads}
    for mask in masks:
        for spot in list(grads):
            grads[spot ^ mask] = swap(grads[spot], mask)
    grads = [grads[spot] for spot in range(dp_size)]

    def columns(step, which):
        return lax.dynamic_slice_in_dim(hidden_acts, (2 * step + which) * BLOCK, BLOCK, 1)

    pieces = []
    for step in range(steps):
        same, other = columns(step, core), columns(step, 1 - core)
        got = {}
        for spot in reversed(range(1, dp_size)):
            got[spot] = swap(other if spot % 2 else same, spot)
        pieces.append([got[spot] for spot in range(1, dp_size)])

    spread = precondition_grads(grads, tokens)
    backs = []
    whole = None
    for step in range(steps):
        back = backs[step - 2] if step >= 2 else None
        whole, send = precondition_block(
            step, tokens, damping, hidden_acts, pieces[step], spread, back, whole
        )
        backs.append(swap(send, 1))
    for step in range(max(steps - 2, 0), steps):
        whole = place(step, backs[step], whole)
    return whole


def solution(mesh):
    def run(hidden_acts, out_grads, damping):
        step = jax.shard_map(
            local,
            mesh=mesh,
            in_specs=(P("dp", "hid"), P("dp", None), P()),
            out_specs=P("hid", None),
            check_vma=False,
        )
        return step(hidden_acts, out_grads, damping)

    return run
```

```python
import functools

import jax
import jax.numpy as jnp
from jax import lax
from jax.experimental import pallas as pl
from jax.experimental.pallas import tpu as pltpu
from jax.sharding import PartitionSpec as P


BLOCK = 1024
ITERS = 3
OUT_DAMPING = 0.1
KERNEL_VMEM = 24 * 2**20
GRAD_CUTS = 4
LATE = 2


ANY = pl.BlockSpec(memory_space=pl.ANY)
VMEM = pl.BlockSpec(memory_space=pltpu.VMEM)
SMEM = pl.BlockSpec(memory_space=pltpu.SMEM)
NN = (((1,), (0,)), ((), ()))
TN = (((0,), (0,)), ((), ()))
TILE = 256


def dot(a, b, dims=NN):
    return lax.dot_general(a, b, dims, preferred_element_type=jnp.float32)


def swap(value, axis, mask):
    pairs = [(source, source ^ mask) for source in range(lax.axis_size(axis))]
    return lax.ppermute(value, axis, pairs)


def aligned(index, size):
    if isinstance(index, int):
        return pl.ds(index * size, size)
    return pl.ds(pl.multiple_of(index * size, size), size)


def gram_tile(pieces, rows, cols):
    value = dot(pieces[0][:, rows], pieces[0][:, cols], TN)
    for piece in pieces[1:]:
        value = value + dot(piece[:, rows], piece[:, cols], TN)
    return value


def upper_gram(pieces, factor):
    for lo in range(0, factor.shape[0], TILE):
        cols, rows = slice(lo, lo + TILE), slice(0, lo + TILE)
        factor[rows, cols] = gram_tile(pieces, rows, cols)


def scaled_factor(pieces, prior, factor, powers, damping, tokens):
    total = jnp.zeros((1, TILE), jnp.float32)
    diagonal = lax.broadcasted_iota(jnp.int32, (TILE, TILE), 0) == lax.broadcasted_iota(
        jnp.int32, (TILE, TILE), 1
    )
    shift = jnp.where(diagonal, damping, 0.0)
    for lo in range(0, factor.shape[0], TILE):
        cols, rows = slice(lo, lo + TILE), slice(0, lo + TILE)
        value = gram_tile(pieces, rows, cols)
        if prior is not None:
            value = value + prior[rows, cols]
        value = value * (1.0 / tokens)
        own = value[lo:] + shift
        factor[cols, cols] = own
        powers[0, cols, cols] = own.astype(jnp.bfloat16)
        total = total + jnp.sum(own * own, axis=0, keepdims=True)
        if lo:
            above = value[:lo]
            factor[:lo, cols] = above
            total = total + 2.0 * jnp.sum(above * above, axis=0, keepdims=True)
            narrow = above.astype(jnp.bfloat16)
            powers[0, :lo, cols] = narrow
            powers[0, cols, :lo] = narrow.T
    return 1.0 / jnp.sqrt(jnp.sum(total, axis=1, keepdims=True))


def residual_powers(factor, scale, powers):
    def square(k, carry):
        first = jnp.where(k == 0, scale, 1.0)
        twice, squared = 2.0 * first, first * first
        for lo in range(0, factor.shape[0], TILE):
            cols, rows = slice(lo, lo + TILE), slice(0, lo + TILE)
            value = twice * factor[rows, cols] - squared * dot(
                powers[k, rows, :], powers[k, :, cols]
            )
            factor[rows, cols] = value
            narrow = value.astype(jnp.bfloat16)
            powers[k + 1, rows, cols] = narrow
            if lo:
                powers[k + 1, cols, :lo] = narrow[:lo].T
        return carry

    lax.fori_loop(0, ITERS - 1, square, 0)


def out_kernel(cuts, tokens, *refs):
    span = tokens // 4
    count = 2 + 2 * cuts
    pieces = refs[:count]
    high_ref, low_ref, grads, factor, powers, wide, sem = refs[count:]
    hid = lax.axis_index("hid")
    small = span // cuts
    starts = [0, span]
    for spot in (2, 3):
        starts += [
            pl.multiple_of(spot * span + lax.rem(hid ^ cut, cuts) * small, small)
            for cut in range(cuts)
        ]
    copies = [
        pltpu.make_async_copy(
            piece, grads.at[pl.ds(start, piece.shape[0])], sem.at[place]
        )
        for place, (piece, start) in enumerate(zip(pieces, starts))
    ]
    start_all(copies)
    wait_all(copies)
    scale = scaled_factor([grads], None, factor, powers, OUT_DAMPING, tokens)
    residual_powers(factor, scale, powers)

    def begin(turn, carry):
        rows = aligned(turn, TILE)
        wide[rows, :] = grads[rows, :].astype(jnp.float32)
        return carry

    lax.fori_loop(0, tokens // TILE, begin, 0)

    def apply(turn, carry):
        last = jnp.where(turn == ITERS - 1, scale, 1.0)
        twice, squared = 2.0 * last, last * last

        def tile(place):
            rows = aligned(place, TILE)
            value = twice * wide[rows, :] - squared * dot(
                grads[rows, :], powers[ITERS - 1 - turn]
            )
            wide[rows, :] = value
            grads[rows, :] = value.astype(jnp.bfloat16)

        in_parts(tokens // TILE, 2, tile)
        return carry

    lax.fori_loop(0, ITERS, apply, 0)

    def finish(turn, carry):
        rows = aligned(turn, TILE)
        high = grads[rows, :]
        high_ref[rows, :] = high
        low_ref[rows, :] = (wide[rows, :] - high.astype(jnp.float32)).astype(jnp.bfloat16)
        return carry

    lax.fori_loop(0, tokens // TILE, finish, 0)


def start_all(copies):
    for copy in copies:
        copy.start()


def wait_all(copies):
    for copy in copies:
        copy.wait()


def precondition_grads(pieces, cuts, tokens):
    width = pieces[0].shape[1]
    return pl.pallas_call(
        functools.partial(out_kernel, cuts, tokens),
        out_shape=[jax.ShapeDtypeStruct((tokens, width), jnp.bfloat16)] * 2,
        in_specs=[VMEM] * len(pieces),
        out_specs=[VMEM] * 2,
        scratch_shapes=[
            pltpu.VMEM((tokens, width), jnp.bfloat16),
            *square_scratch(width),
            pltpu.SemaphoreType.DMA((len(pieces),)),
        ],
        compiler_params=pltpu.CompilerParams(vmem_limit_bytes=KERNEL_VMEM),
        name="out_side",
    )(*pieces)


def square_scratch(width):
    return [
        pltpu.VMEM((BLOCK, BLOCK), jnp.float32),
        pltpu.VMEM((ITERS, BLOCK, BLOCK), jnp.bfloat16),
        pltpu.VMEM((BLOCK, width), jnp.float32),
    ]


def place_copies(source, whole_ref, block, sems, parts=4):
    span = BLOCK // parts
    return [
        pltpu.make_async_copy(
            source.at[pl.ds(part * span, span)],
            whole_ref.at[aligned(block * parts + part, span)],
            sems.at[part],
        )
        for part in range(parts)
    ]


def in_parts(count, parts, body):
    if parts == 1:
        for place in range(count):
            body(place)
        return
    inner = count // parts

    def turn(part, carry):
        for place in range(inner):
            body(part * inner + place)
        return carry

    lax.fori_loop(0, parts, turn, 0)


def right_side(pieces, spots, spread, prior, scale, wide, narrow, parts):
    span = pieces[0].shape[0]

    def tile(place):
        rows = aligned(place, TILE)
        value = prior[rows, :] if prior is not None else None
        for spot, piece in zip(spots, pieces):
            for part in spread:
                term = dot(piece[:, rows], part[spot * span : (spot + 1) * span, :], TN)
                value = term if value is None else value + term
        if scale is not None:
            value = value * scale
        wide[rows, :] = value
        if narrow is not None:
            narrow[rows, :] = value.astype(jnp.bfloat16)

    in_parts(BLOCK // TILE, parts, tile)


def apply_powers(powers, scale, wide, narrow, parts):
    def apply(turn, carry):
        last = jnp.where(turn == ITERS - 1, scale, 1.0)

        def tile(place):
            cols = aligned(place, TILE)
            value = 2.0 * wide[:, cols] - last * dot(
                powers[ITERS - 1 - turn], narrow[:, cols]
            )
            wide[:, cols] = value
            narrow[:, cols] = value.astype(jnp.bfloat16)

        in_parts(wide.shape[1] // TILE, parts, tile)
        return carry

    lax.fori_loop(0, ITERS, apply, 0)


def block_damping(damping_ref, step, blocks):
    return damping_ref[
        lax.axis_index("hid") * blocks + 2 * step + lax.axis_index("dp") % 2
    ]


def moves(places, refs, whole_ref, sem):
    core = lax.axis_index("dp") % 2
    copies = []
    for turn, (own, back) in enumerate(places):
        block = 2 * back + (core if own else 1 - core)
        copies += place_copies(refs[turn], whole_ref, block, sem.at[turn])
    return copies


def block_kernel(parts_at, step, blocks, tokens, spots, places, held, damping_ref, *refs):
    parts = len(spots)
    pieces, spread, refs = refs[:parts], refs[parts : parts + 2], refs[parts + 2 :]
    moving, refs = refs[: len(places)], refs[len(places) + held :]
    whole_ref, send_ref, factor, powers, wide, sem = refs
    copies = moves(places, moving, whole_ref, sem)
    start_all(copies)
    damping = block_damping(damping_ref, step, blocks)
    scale = scaled_factor(pieces, None, factor, powers, damping, tokens)
    residual_powers(factor, scale, powers)
    right_side(pieces, spots, spread, None, scale, wide, send_ref, 2)
    apply_powers(powers, scale, wide, send_ref, parts_at)
    wait_all(copies)


def early_kernel(step, blocks, tokens, spots, places, held, *refs):
    parts = len(spots)
    pieces, spread, refs = refs[:parts], refs[parts : parts + 2], refs[parts + 2 :]
    moving, refs = refs[: len(places)], refs[len(places) + held :]
    whole_ref, gram_ref, right_ref, sem = refs
    copies = moves(places, moving, whole_ref, sem)
    start_all(copies)
    upper_gram(pieces, gram_ref)
    right_side(pieces, spots, spread, None, None, right_ref, None, 2)
    wait_all(copies)


def late_kernel(step, blocks, tokens, spots, places, held, damping_ref, *refs):
    parts = len(spots)
    pieces, spread, refs = refs[:parts], refs[parts : parts + 2], refs[parts + 2 :]
    gram_ref, right_ref, refs = *refs[:2], refs[2:]
    moving, refs = refs[: len(places)], refs[len(places) + held :]
    whole_ref, send_ref, factor, powers, wide, sem = refs
    copies = moves(places, moving, whole_ref, sem)
    start_all(copies)
    damping = block_damping(damping_ref, step, blocks)
    scale = scaled_factor(pieces, gram_ref, factor, powers, damping, tokens)
    residual_powers(factor, scale, powers)
    right_side(pieces, spots, spread, right_ref, scale, wide, send_ref, 2)
    apply_powers(powers, scale, wide, send_ref, 1)
    wait_all(copies)


def call(kernel, operands, specs, outs, out_specs, scratch_shapes, held):
    return pl.pallas_call(
        kernel,
        out_shape=outs,
        in_specs=specs,
        out_specs=out_specs,
        input_output_aliases={len(operands) - 1: 0} if held else {},
        scratch_shapes=scratch_shapes,
        compiler_params=pltpu.CompilerParams(vmem_limit_bytes=KERNEL_VMEM),
    )(*operands)


def block_call(kernel, step, blocks, tokens, damping, pieces, spread, extra, moving, whole):
    width = spread[0].shape[1]
    spots = sorted(pieces)
    held = whole is not None
    operands = [pieces[spot] for spot in spots] + [*spread, *extra, *moving.values()]
    specs = [VMEM] * len(operands)
    if damping is not None:
        operands, specs = [damping] + operands, [SMEM] + specs
    if held:
        operands, specs = operands + [whole], specs + [ANY]
    rows = blocks * BLOCK
    outs = [jax.ShapeDtypeStruct((rows, width), jnp.bfloat16)]
    if damping is None:
        outs.append(jax.ShapeDtypeStruct((BLOCK, BLOCK), jnp.float32))
        outs.append(jax.ShapeDtypeStruct((BLOCK, width), jnp.float32))
        shapes = []
    else:
        outs.append(jax.ShapeDtypeStruct((BLOCK, width), jnp.bfloat16))
        shapes = square_scratch(width)
    shapes = shapes + [pltpu.SemaphoreType.DMA((2, 4))]
    kernel = functools.partial(kernel, step, blocks, tokens, spots, list(moving), held)
    out_specs = [ANY] + [VMEM] * (len(outs) - 1)
    return call(kernel, operands, specs, outs, out_specs, shapes, held)


def place_kernel(step, own, source, held_ref, whole_ref, sem):
    core = lax.axis_index("dp") % 2
    copies = place_copies(source, whole_ref, 2 * step + (core if own else 1 - core), sem, 8)
    start_all(copies)
    wait_all(copies)


def place(step, own, source, whole):
    return call(
        functools.partial(place_kernel, step, own),
        [source, whole],
        [VMEM, ANY],
        jax.ShapeDtypeStruct(whole.shape, whole.dtype),
        ANY,
        [pltpu.SemaphoreType.DMA((8,))],
        True,
    )


def local(cuts, hidden_acts, out_grads, damping):
    span = hidden_acts.shape[0]
    tokens = span * lax.axis_size("dp")
    core = lax.axis_index("dp") % 2
    blocks = hidden_acts.shape[1] // BLOCK
    steps = blocks // 2
    spots = range(1, lax.axis_size("dp"))

    small = span // cuts
    part = lax.dynamic_slice_in_dim(out_grads, lax.axis_index("hid") % cuts * small, small, 0)
    over = [swap(part, "dp", LATE)]
    over += [swap(over[0], "hid", cut) for cut in range(1, cuts)]
    side = swap(out_grads, "dp", 1)
    cross = [swap(over[cut], "dp", 1) for cut in range(cuts)]

    def columns(step, which):
        return lax.dynamic_slice_in_dim(hidden_acts, (2 * step + which) * BLOCK, BLOCK, 1)

    pieces = []
    for step in range(steps):
        same, other = columns(step, core), columns(step, 1 - core)
        pieces.append({0: same})
        for spot in spots:
            pieces[step][spot] = swap(other if spot % 2 else same, "dp", spot)

    spread = precondition_grads([out_grads, side, *over, *cross], cuts, tokens)
    sends, backs = [], []
    whole = None

    def moving(step):
        ready = {}
        if 1 <= step <= len(sends):
            ready[True, step - 1] = sends[step - 1]
        if step >= 2:
            ready[False, step - 2] = backs[step - 2]
        return ready

    for step in range(steps - 1):
        whole, send = block_call(
            functools.partial(block_kernel, 1), step, blocks, tokens, damping, pieces[step], spread, (),
            moving(step), whole,
        )
        sends.append(send)
        backs.append(swap(send, "dp", 1))
    step = steps - 1
    late = {LATE: pieces[step].pop(LATE)}
    whole, gram, right = block_call(
        early_kernel, step, blocks, tokens, None, pieces[step], spread, (),
        moving(step), whole,
    )
    ready = {(False, step - 1): backs[step - 1]} if step else {}
    whole, send = block_call(
        late_kernel, step, blocks, tokens, damping, late, spread, (gram, right),
        ready, whole,
    )
    last = swap(send, "dp", 1)
    whole = place(step, True, send, whole)
    return place(step, False, last, whole)


def solution(mesh):
    hid_size = mesh.shape["hid"]
    cuts = min(GRAD_CUTS, hid_size & -hid_size)

    def body(hidden_acts, out_grads, damping):
        return local(cuts, hidden_acts, out_grads, damping)

    def run(hidden_acts, out_grads, damping):
        step = jax.shard_map(
            body,
            mesh=mesh,
            in_specs=(P("dp", "hid"), P("dp", None), P()),
            out_specs=P("hid", None),
            check_vma=False,
        )
        return step(hidden_acts, out_grads, damping)

    return run
```

```python
import functools

import jax
import jax.numpy as jnp
from jax import lax
from jax.experimental import pallas as pl
from jax.experimental.pallas import tpu as pltpu
from jax.sharding import PartitionSpec as P


BLOCK = 1024
ITERS = 3
OUT_DAMPING = 0.1
KERNEL_VMEM = 24 * 2**20
GRAD_CUTS = 4
LATE = 2


ANY = pl.BlockSpec(memory_space=pl.ANY)
VMEM = pl.BlockSpec(memory_space=pltpu.VMEM)
SMEM = pl.BlockSpec(memory_space=pltpu.SMEM)
NN = (((1,), (0,)), ((), ()))
TN = (((0,), (0,)), ((), ()))
TILE = 256
PLACE_PARTS = 4
SOLO_CUTS = (3 * BLOCK // 4, BLOCK // 4)


def dot(a, b, dims=NN):
    return lax.dot_general(a, b, dims, preferred_element_type=jnp.float32)


def swap(value, axis, mask):
    pairs = [(source, source ^ mask) for source in range(lax.axis_size(axis))]
    return lax.ppermute(value, axis, pairs)


def aligned(index, size):
    if isinstance(index, int):
        return pl.ds(index * size, size)
    return pl.ds(pl.multiple_of(index * size, size), size)


def gram_tile(pieces, rows, cols):
    value = dot(pieces[0][:, rows], pieces[0][:, cols], TN)
    for piece in pieces[1:]:
        value = value + dot(piece[:, rows], piece[:, cols], TN)
    return value


def upper_gram(pieces, factor):
    for lo in range(0, factor.shape[0], TILE):
        cols, rows = slice(lo, lo + TILE), slice(0, lo + TILE)
        factor[rows, cols] = gram_tile(pieces, rows, cols)


def scaled_factor(pieces, prior, factor, powers, damping, tokens):
    total = jnp.zeros((1, TILE), jnp.float32)
    diagonal = lax.broadcasted_iota(jnp.int32, (TILE, TILE), 0) == lax.broadcasted_iota(
        jnp.int32, (TILE, TILE), 1
    )
    shift = jnp.where(diagonal, damping, 0.0)
    for lo in range(0, factor.shape[0], TILE):
        cols, rows = slice(lo, lo + TILE), slice(0, lo + TILE)
        value = gram_tile(pieces, rows, cols)
        if prior is not None:
            value = value + prior[rows, cols]
        value = value * (1.0 / tokens)
        own = value[lo:] + shift
        factor[cols, cols] = own
        powers[0, cols, cols] = own.astype(jnp.bfloat16)
        total = total + jnp.sum(own * own, axis=0, keepdims=True)
        if lo:
            above = value[:lo]
            factor[:lo, cols] = above
            total = total + 2.0 * jnp.sum(above * above, axis=0, keepdims=True)
            narrow = above.astype(jnp.bfloat16)
            powers[0, :lo, cols] = narrow
            powers[0, cols, :lo] = narrow.T
    return 1.0 / jnp.sqrt(jnp.sum(total, axis=1, keepdims=True))


def residual_powers(factor, scale, powers):
    def square(k, carry):
        first = jnp.where(k == 0, scale, 1.0)
        twice, squared = 2.0 * first, first * first
        for lo in range(0, factor.shape[0], TILE):
            cols, rows = slice(lo, lo + TILE), slice(0, lo + TILE)
            value = twice * factor[rows, cols] - squared * dot(
                powers[k, rows, :], powers[k, :, cols]
            )
            factor[rows, cols] = value
            narrow = value.astype(jnp.bfloat16)
            powers[k + 1, rows, cols] = narrow
            if lo:
                powers[k + 1, cols, :lo] = narrow[:lo].T
        return carry

    lax.fori_loop(0, ITERS - 1, square, 0)


def out_kernel(cuts, tokens, *refs):
    span = tokens // 4
    count = 2 + 2 * cuts
    pieces = refs[:count]
    grads, powers, scale_ref, factor, sem = refs[count:]
    hid = lax.axis_index("hid")
    small = span // cuts
    starts = [0, span]
    for spot in (2, 3):
        starts += [
            pl.multiple_of(spot * span + lax.rem(hid ^ cut, cuts) * small, small)
            for cut in range(cuts)
        ]
    copies = [
        pltpu.make_async_copy(
            piece, grads.at[pl.ds(start, piece.shape[0])], sem.at[place]
        )
        for place, (piece, start) in enumerate(zip(pieces, starts))
    ]
    start_all(copies)
    wait_all(copies)
    scale = scaled_factor([grads], None, factor, powers, OUT_DAMPING, tokens)
    scale_ref[...] = jnp.broadcast_to(scale, scale_ref.shape)
    residual_powers(factor, scale, powers)


def spread_kernel(tokens, given, powers, scale_ref, *refs):
    high_ref, low_ref, high_half, low_half, grads, wide = refs
    scale = scale_ref[:1, :1]
    left = lax.axis_index("dp") % 2 == 0
    half = wide.shape[1] // 2

    def begin(turn, carry):
        rows = aligned(turn, TILE)
        value = given[rows, :]
        grads[rows, :] = value
        wide[rows, :] = value.astype(jnp.float32)
        return carry

    lax.fori_loop(0, tokens // TILE, begin, 0)

    def apply(turn, carry):
        last = jnp.where(turn == ITERS - 1, scale, 1.0)
        twice, squared = 2.0 * last, last * last

        def tile(place):
            rows = aligned(place, TILE)
            value = twice * wide[rows, :] - squared * dot(
                grads[rows, :], powers[ITERS - 1 - turn]
            )
            wide[rows, :] = value
            grads[rows, :] = value.astype(jnp.bfloat16)

        in_parts(tokens // TILE, 1, tile)
        return carry

    lax.fori_loop(0, ITERS, apply, 0)

    def finish(turn, carry):
        rows = aligned(turn, TILE)
        high = grads[rows, :]
        low = (wide[rows, :] - high.astype(jnp.float32)).astype(jnp.bfloat16)
        high_ref[rows, :] = high
        low_ref[rows, :] = low
        high_half[rows, :] = jnp.where(left, high[:, :half], high[:, half:])
        low_half[rows, :] = jnp.where(left, low[:, :half], low[:, half:])
        return carry

    lax.fori_loop(0, tokens // TILE, finish, 0)


def start_all(copies):
    for copy in copies:
        copy.start()


def wait_all(copies):
    for copy in copies:
        copy.wait()


def out_factor_powers(pieces, cuts, tokens):
    width = pieces[0].shape[1]
    return pl.pallas_call(
        functools.partial(out_kernel, cuts, tokens),
        out_shape=[
            jax.ShapeDtypeStruct((tokens, width), jnp.bfloat16),
            jax.ShapeDtypeStruct((ITERS, width, width), jnp.bfloat16),
            jax.ShapeDtypeStruct((8, 128), jnp.float32),
        ],
        in_specs=[VMEM] * len(pieces),
        out_specs=[VMEM] * 3,
        scratch_shapes=[
            pltpu.VMEM((width, width), jnp.float32),
            pltpu.SemaphoreType.DMA((len(pieces),)),
        ],
        compiler_params=pltpu.CompilerParams(vmem_limit_bytes=KERNEL_VMEM),
        name="out_factor",
    )(*pieces)


def precondition_grads(grads, powers, scale):
    tokens, width = grads.shape
    return pl.pallas_call(
        functools.partial(spread_kernel, tokens),
        out_shape=[jax.ShapeDtypeStruct((tokens, width), jnp.bfloat16)] * 2
        + [jax.ShapeDtypeStruct((tokens, width // 2), jnp.bfloat16)] * 2,
        in_specs=[VMEM] * 3,
        out_specs=[VMEM] * 4,
        scratch_shapes=[
            pltpu.VMEM((tokens, width), jnp.bfloat16),
            pltpu.VMEM((tokens, width), jnp.float32),
        ],
        compiler_params=pltpu.CompilerParams(vmem_limit_bytes=KERNEL_VMEM),
        name="out_spread",
    )(grads, powers, scale)


def square_scratch(width):
    return [
        pltpu.VMEM((BLOCK, BLOCK), jnp.float32),
        pltpu.VMEM((ITERS, BLOCK, BLOCK), jnp.bfloat16),
        pltpu.VMEM((BLOCK, width), jnp.float32),
    ]


def place_copies(places, refs, whole_ref, sem):
    core = lax.axis_index("dp") % 2
    chip = lax.axis_index("dp") // 2 % 2
    copies = []
    for (kind, first, second, *rest), ref in zip(places, refs):
        if kind == "full":
            block = 2 * second + (core if first else 1 - core)
            pieces, base, columns = PLACE_PARTS, 0, slice(None)
        else:
            block = whole_ref.shape[0] // BLOCK - 2 + (chip if first else 1 - chip)
            pieces, base = 1, rest[0]
            columns = aligned(core if second else 1 - core, ref.shape[1])
        span = ref.shape[0] // pieces
        for piece in range(pieces):
            rows = pl.ds(pl.multiple_of(block * BLOCK + base + piece * span, BLOCK // 8), span)
            copies.append(
                pltpu.make_async_copy(
                    ref.at[pl.ds(piece * span, span)],
                    whole_ref.at[rows, columns],
                    sem.at[len(copies)],
                )
            )
    return copies


def place_count(places):
    return max(1, sum(PLACE_PARTS if kind == "full" else 1 for kind, *_ in places))


def in_parts(count, parts, body):
    if parts == 1:
        for place in range(count):
            body(place)
        return
    inner = count // parts

    def turn(part, carry):
        for place in range(inner):
            body(part * inner + place)
        return carry

    lax.fori_loop(0, parts, turn, 0)


def right_side(pieces, spots, spread, prior, scale, wide, narrow, parts):
    span = pieces[0].shape[0]

    def tile(place):
        rows = aligned(place, TILE)
        value = prior[rows, :] if prior is not None else None
        for spot, piece in zip(spots, pieces):
            for part in spread:
                term = dot(piece[:, rows], part[spot * span : (spot + 1) * span, :], TN)
                value = term if value is None else value + term
        if scale is not None:
            value = value * scale
        wide[rows, :] = value
        if narrow is not None:
            narrow[rows, :] = value.astype(jnp.bfloat16)

    in_parts(BLOCK // TILE, parts, tile)


def apply_powers(powers, scale, wide, narrow):
    def apply(turn, carry):
        last = jnp.where(turn == ITERS - 1, scale, 1.0)
        for lo in range(0, wide.shape[1], TILE):
            cols = slice(lo, lo + TILE)
            value = 2.0 * wide[:, cols] - last * dot(
                powers[ITERS - 1 - turn], narrow[:, cols]
            )
            wide[:, cols] = value
            narrow[:, cols] = value.astype(jnp.bfloat16)
        return carry

    lax.fori_loop(0, ITERS, apply, 0)


def block_damping(damping_ref, block, blocks):
    return damping_ref[lax.axis_index("hid") * blocks + block]


def own_block(step):
    return 2 * step + lax.axis_index("dp") % 2


def block_kernel(step, blocks, tokens, spots, places, held, damping_ref, *refs):
    parts = len(spots)
    pieces, spread, refs = refs[:parts], refs[parts : parts + 2], refs[parts + 2 :]
    moving, refs = refs[: len(places)], refs[len(places) + held :]
    whole_ref, send_ref, factor, powers, wide, sem = refs
    copies = place_copies(places, moving, whole_ref, sem)
    start_all(copies)
    damping = block_damping(damping_ref, own_block(step), blocks)
    scale = scaled_factor(pieces, None, factor, powers, damping, tokens)
    residual_powers(factor, scale, powers)
    right_side(pieces, spots, spread, None, scale, wide, send_ref, 2)
    apply_powers(powers, scale, wide, send_ref)
    wait_all(copies)


def solo_kernel(step, blocks, tokens, spots, places, held, damping_ref, *refs):
    parts = len(spots)
    pieces, spread, refs = refs[:parts], refs[parts : parts + 2], refs[parts + 2 :]
    whole_ref, half_ref, *cut_refs = refs[:-4]
    factor, powers, wide, _ = refs[-4:]
    block = blocks - 2 + lax.axis_index("dp") // 2 % 2
    damping = block_damping(damping_ref, block, blocks)
    scale = scaled_factor(pieces, None, factor, powers, damping, tokens)
    residual_powers(factor, scale, powers)
    right_side(pieces, spots, spread, None, scale, wide, half_ref, 2)
    apply_powers(powers, scale, wide, half_ref)
    row = 0
    for cut_ref in cut_refs:
        cut_ref[...] = half_ref[row : row + cut_ref.shape[0], :]
        row += cut_ref.shape[0]


def early_kernel(step, blocks, tokens, spots, places, held, *refs):
    parts = len(spots)
    pieces, spread, refs = refs[:parts], refs[parts : parts + 2], refs[parts + 2 :]
    moving, refs = refs[: len(places)], refs[len(places) + held :]
    whole_ref, gram_ref, right_ref, sem = refs
    copies = place_copies(places, moving, whole_ref, sem)
    start_all(copies)
    upper_gram(pieces, gram_ref)
    right_side(pieces, spots, spread, None, None, right_ref, None, 2)
    wait_all(copies)


def late_kernel(step, blocks, tokens, spots, places, held, damping_ref, *refs):
    parts = len(spots)
    pieces, spread, refs = refs[:parts], refs[parts : parts + 2], refs[parts + 2 :]
    gram_ref, right_ref, refs = *refs[:2], refs[2:]
    moving, refs = refs[: len(places)], refs[len(places) + held :]
    whole_ref, send_ref, factor, powers, wide, sem = refs
    copies = place_copies(places, moving, whole_ref, sem)
    start_all(copies)
    damping = block_damping(damping_ref, own_block(step), blocks)
    scale = scaled_factor(pieces, gram_ref, factor, powers, damping, tokens)
    residual_powers(factor, scale, powers)
    right_side(pieces, spots, spread, right_ref, scale, wide, send_ref, 2)
    apply_powers(powers, scale, wide, send_ref)
    wait_all(copies)


def call(kernel, operands, specs, outs, out_specs, scratch_shapes, held):
    return pl.pallas_call(
        kernel,
        out_shape=outs,
        in_specs=specs,
        out_specs=out_specs,
        input_output_aliases={len(operands) - 1: 0} if held else {},
        scratch_shapes=scratch_shapes,
        compiler_params=pltpu.CompilerParams(vmem_limit_bytes=KERNEL_VMEM),
    )(*operands)


def block_call(kernel, name, step, blocks, tokens, damping, pieces, spread, extra, moving, whole):
    width = spread[0].shape[1]
    spots = sorted(pieces)
    held = whole is not None
    operands = [pieces[spot] for spot in spots] + [*spread, *extra, *moving.values()]
    specs = [VMEM] * len(operands)
    if damping is not None:
        operands, specs = [damping] + operands, [SMEM] + specs
    if held:
        operands, specs = operands + [whole], specs + [ANY]
    rows = blocks * BLOCK
    full = width * (2 if name == "solo" else 1)
    outs = [jax.ShapeDtypeStruct((rows, full), jnp.bfloat16)]
    if damping is None:
        outs.append(jax.ShapeDtypeStruct((BLOCK, BLOCK), jnp.float32))
        outs.append(jax.ShapeDtypeStruct((BLOCK, width), jnp.float32))
        shapes = []
    else:
        outs.append(jax.ShapeDtypeStruct((BLOCK, width), jnp.bfloat16))
        shapes = square_scratch(width)
    if name == "solo":
        outs += [jax.ShapeDtypeStruct((rows, width), jnp.bfloat16) for rows in SOLO_CUTS]
    places = list(moving)
    shapes = shapes + [pltpu.SemaphoreType.DMA((place_count(places),))]
    kernel = functools.partial(kernel, step, blocks, tokens, spots, places, held)
    out_specs = [ANY] + [VMEM] * (len(outs) - 1)
    return call(kernel, operands, specs, outs, out_specs, shapes, held)


def place_kernel(places, *refs):
    count = len(places)
    whole_ref, sem = refs[count + 1 :]
    copies = place_copies(places, refs[:count], whole_ref, sem)
    start_all(copies)
    wait_all(copies)


def place(moving, whole):
    places = list(moving)
    return call(
        functools.partial(place_kernel, places),
        [*moving.values(), whole],
        [VMEM] * len(places) + [ANY],
        jax.ShapeDtypeStruct(whole.shape, whole.dtype),
        ANY,
        [pltpu.SemaphoreType.DMA((place_count(places),))],
        True,
    )


def local(cuts, hidden_acts, out_grads, damping):
    span = hidden_acts.shape[0]
    tokens = span * lax.axis_size("dp")
    core = lax.axis_index("dp") % 2
    chip = lax.axis_index("dp") // 2 % 2
    blocks = hidden_acts.shape[1] // BLOCK
    steps = step_count(blocks)
    spots = range(1, lax.axis_size("dp"))

    small = span // cuts
    part = lax.dynamic_slice_in_dim(out_grads, lax.axis_index("hid") % cuts * small, small, 0)
    over = [swap(part, "dp", LATE)]
    over += [swap(over[0], "hid", cut) for cut in range(1, cuts)]
    side = swap(out_grads, "dp", 1)
    cross = [swap(over[cut], "dp", 1) for cut in range(cuts)]

    def columns(block):
        return lax.dynamic_slice_in_dim(hidden_acts, block * BLOCK, BLOCK, 1)

    if steps * 2 < blocks:
        mine, theirs = columns(blocks - 2 + chip), columns(blocks - 1 - chip)
        solo = {0: mine, 1: swap(mine, "dp", 1), 2: swap(theirs, "dp", 2)}
        solo[3] = swap(solo[2], "dp", 1)
    pieces = []
    for step in range(steps):
        same, other = columns(2 * step + core), columns(2 * step + 1 - core)
        pieces.append({0: same})
        for spot in spots:
            pieces[step][spot] = swap(other if spot % 2 else same, "dp", spot)

    factor = out_factor_powers([out_grads, side, *over, *cross], cuts, tokens)
    high, low, high_half, low_half = precondition_grads(*factor)
    spread = (high, low)
    whole = None
    ready, final = {}, [{} for _ in range(2)]
    if steps * 2 < blocks:
        whole, half, *parts = block_call(
            solo_kernel, "solo", None, blocks, tokens, damping, solo, (high_half, low_half),
            (), {}, None,
        )
        ready["half", True, True, 0] = half
        upcoming = {("half", True, False, 0): swap(half, "dp", 1)}
        final += [{}, {}]
        row = 0
        for turn, part in enumerate(parts):
            got = swap(part, "dp", 2)
            passed = swap(got, "dp", 1)
            final[2]["half", False, True, row] = got
            final[turn + 2]["half", False, False, row] = passed
            row += part.shape[0]
    else:
        upcoming = {}
    for step in range(steps - 1):
        whole, send = block_call(
            block_kernel, "block", step, blocks, tokens, damping, pieces[step], spread, (),
            ready, whole,
        )
        ready = {("full", True, step): send, **upcoming}
        upcoming = {("full", False, step): swap(send, "dp", 1)}
    step = steps - 1
    late = {LATE: pieces[step].pop(LATE)}
    whole, gram, right = block_call(
        early_kernel, "early", step, blocks, tokens, None, pieces[step], spread, (),
        ready, whole,
    )
    whole, send = block_call(
        late_kernel, "late", step, blocks, tokens, damping, late, spread, (gram, right),
        upcoming, whole,
    )
    final[0]["full", True, step] = send
    final[1]["full", False, step] = swap(send, "dp", 1)
    for moving in final:
        whole = place(moving, whole)
    return whole


def step_count(blocks):
    return (blocks - 2) // 2 if blocks > 4 else blocks // 2


def solution(mesh):
    hid_size = mesh.shape["hid"]
    cuts = min(GRAD_CUTS, hid_size & -hid_size)

    def body(hidden_acts, out_grads, damping):
        return local(cuts, hidden_acts, out_grads, damping)

    def run(hidden_acts, out_grads, damping):
        step = jax.shard_map(
            body,
            mesh=mesh,
            in_specs=(P("dp", "hid"), P("dp", None), P()),
            out_specs=P("hid", None),
            check_vma=False,
        )
        return step(hidden_acts, out_grads, damping)

    return run
```

```python
import functools

import jax
import jax.numpy as jnp
from jax import lax
from jax.experimental import pallas as pl
from jax.experimental.pallas import tpu as pltpu
from jax.sharding import PartitionSpec as P


BLOCK = 1024
ITERS = 3
OUT_DAMPING = 0.1
KERNEL_VMEM = 24 * 2**20
GRAD_CUTS = 4
LATE = 2


ANY = pl.BlockSpec(memory_space=pl.ANY)
VMEM = pl.BlockSpec(memory_space=pltpu.VMEM)
SMEM = pl.BlockSpec(memory_space=pltpu.SMEM)
NN = (((1,), (0,)), ((), ()))
TN = (((0,), (0,)), ((), ()))
TILE = 256
PLACE_PARTS = 4
SOLO_CUTS = (3 * BLOCK // 4, BLOCK // 4)


def dot(a, b, dims=NN):
    return lax.dot_general(a, b, dims, preferred_element_type=jnp.float32)


def swap(value, axis, mask):
    pairs = [(source, source ^ mask) for source in range(lax.axis_size(axis))]
    return lax.ppermute(value, axis, pairs)


def aligned(index, size):
    if isinstance(index, int):
        return pl.ds(index * size, size)
    return pl.ds(pl.multiple_of(index * size, size), size)


def gram_tile(pieces, rows, cols):
    value = dot(pieces[0][:, rows], pieces[0][:, cols], TN)
    for piece in pieces[1:]:
        value = value + dot(piece[:, rows], piece[:, cols], TN)
    return value


def upper_gram(pieces, factor):
    for lo in range(0, factor.shape[0], TILE):
        cols, rows = slice(lo, lo + TILE), slice(0, lo + TILE)
        factor[rows, cols] = gram_tile(pieces, rows, cols)


def scaled_factor(pieces, prior, factor, powers, damping, tokens):
    total = jnp.zeros((1, TILE), jnp.float32)
    diagonal = lax.broadcasted_iota(jnp.int32, (TILE, TILE), 0) == lax.broadcasted_iota(
        jnp.int32, (TILE, TILE), 1
    )
    shift = jnp.where(diagonal, damping, 0.0)
    for lo in range(0, factor.shape[0], TILE):
        cols, rows = slice(lo, lo + TILE), slice(0, lo + TILE)
        value = gram_tile(pieces, rows, cols)
        if prior is not None:
            value = value + prior[rows, cols]
        value = value * (1.0 / tokens)
        own = value[lo:] + shift
        factor[cols, cols] = own
        powers[0, cols, cols] = own.astype(jnp.bfloat16)
        total = total + jnp.sum(own * own, axis=0, keepdims=True)
        if lo:
            above = value[:lo]
            factor[:lo, cols] = above
            total = total + 2.0 * jnp.sum(above * above, axis=0, keepdims=True)
            narrow = above.astype(jnp.bfloat16)
            powers[0, :lo, cols] = narrow
            powers[0, cols, :lo] = narrow.T
    return 1.0 / jnp.sqrt(jnp.sum(total, axis=1, keepdims=True))


def residual_powers(factor, scale, powers):
    def square(k, carry):
        first = jnp.where(k == 0, scale, 1.0)
        twice, squared = 2.0 * first, first * first
        for lo in range(0, factor.shape[0], TILE):
            cols, rows = slice(lo, lo + TILE), slice(0, lo + TILE)
            value = twice * factor[rows, cols] - squared * dot(
                powers[k, rows, :], powers[k, :, cols]
            )
            factor[rows, cols] = value
            narrow = value.astype(jnp.bfloat16)
            powers[k + 1, rows, cols] = narrow
            if lo:
                powers[k + 1, cols, :lo] = narrow[:lo].T
        return carry

    lax.fori_loop(0, ITERS - 1, square, 0)


def out_kernel(cuts, tokens, begun, *refs):
    span = tokens // 4
    count = 2 + 2 * cuts
    pieces = refs[:count]
    prior = refs[count] if begun else None
    grads, powers, scale_ref, factor, sem = refs[count + begun :]
    hid = lax.axis_index("hid")
    small = span // cuts
    starts = [0, span]
    for spot in (2, 3):
        starts += [
            pl.multiple_of(spot * span + lax.rem(hid ^ cut, cuts) * small, small)
            for cut in range(cuts)
        ]
    copies = [
        pltpu.make_async_copy(
            piece, grads.at[pl.ds(start, piece.shape[0])], sem.at[place]
        )
        for place, (piece, start) in enumerate(zip(pieces, starts))
    ]
    start_all(copies)
    wait_all(copies)
    left = [grads.at[2 * span :]] if begun else [grads]
    scale = scaled_factor(left, prior, factor, powers, OUT_DAMPING, tokens)
    scale_ref[...] = jnp.broadcast_to(scale, scale_ref.shape)
    residual_powers(factor, scale, powers)


def spread_kernel(tokens, given, powers, scale_ref, *refs):
    high_ref, low_ref, high_half, low_half, grads, wide = refs
    scale = scale_ref[:1, :1]
    left = lax.axis_index("dp") % 2 == 0
    half = wide.shape[1] // 2

    def begin(turn, carry):
        rows = aligned(turn, TILE)
        value = given[rows, :]
        grads[rows, :] = value
        wide[rows, :] = value.astype(jnp.float32)
        return carry

    lax.fori_loop(0, tokens // TILE, begin, 0)

    def apply(turn, carry):
        last = jnp.where(turn == ITERS - 1, scale, 1.0)
        twice, squared = 2.0 * last, last * last

        def tile(place):
            rows = aligned(place, TILE)
            value = twice * wide[rows, :] - squared * dot(
                grads[rows, :], powers[ITERS - 1 - turn]
            )
            wide[rows, :] = value
            grads[rows, :] = value.astype(jnp.bfloat16)

        in_parts(tokens // TILE, 1, tile)
        return carry

    lax.fori_loop(0, ITERS, apply, 0)

    def finish(turn, carry):
        rows = aligned(turn, TILE)
        high = grads[rows, :]
        low = (wide[rows, :] - high.astype(jnp.float32)).astype(jnp.bfloat16)
        high_ref[rows, :] = high
        low_ref[rows, :] = low
        high_half[rows, :] = jnp.where(left, high[:, :half], high[:, half:])
        low_half[rows, :] = jnp.where(left, low[:, :half], low[:, half:])
        return carry

    lax.fori_loop(0, tokens // TILE, finish, 0)


def start_all(copies):
    for copy in copies:
        copy.start()


def wait_all(copies):
    for copy in copies:
        copy.wait()


def out_factor_powers(pieces, prior, cuts, tokens):
    width = pieces[0].shape[1]
    operands = [*pieces, *prior]
    return pl.pallas_call(
        functools.partial(out_kernel, cuts, tokens, len(prior)),
        out_shape=[
            jax.ShapeDtypeStruct((tokens, width), jnp.bfloat16),
            jax.ShapeDtypeStruct((ITERS, width, width), jnp.bfloat16),
            jax.ShapeDtypeStruct((8, 128), jnp.float32),
        ],
        in_specs=[VMEM] * len(operands),
        out_specs=[VMEM] * 3,
        scratch_shapes=[
            pltpu.VMEM((width, width), jnp.float32),
            pltpu.SemaphoreType.DMA((len(pieces),)),
        ],
        compiler_params=pltpu.CompilerParams(vmem_limit_bytes=KERNEL_VMEM),
        name="out_factor",
    )(*operands)


def begin_kernel(*refs):
    count = len(refs) // 3
    for place in range(count):
        upper_gram(refs[2 * place : 2 * place + 2], refs[2 * count + place])


def begin_grams(pairs):
    operands = [piece for pair in pairs for piece in pair]
    width = operands[0].shape[1]
    return pl.pallas_call(
        begin_kernel,
        out_shape=[jax.ShapeDtypeStruct((width, width), jnp.float32)] * len(pairs),
        in_specs=[VMEM] * len(operands),
        out_specs=[VMEM] * len(pairs),
        compiler_params=pltpu.CompilerParams(vmem_limit_bytes=KERNEL_VMEM),
        name="begin",
    )(*operands)


def precondition_grads(grads, powers, scale):
    tokens, width = grads.shape
    return pl.pallas_call(
        functools.partial(spread_kernel, tokens),
        out_shape=[jax.ShapeDtypeStruct((tokens, width), jnp.bfloat16)] * 2
        + [jax.ShapeDtypeStruct((tokens, width // 2), jnp.bfloat16)] * 2,
        in_specs=[VMEM] * 3,
        out_specs=[VMEM] * 4,
        scratch_shapes=[
            pltpu.VMEM((tokens, width), jnp.bfloat16),
            pltpu.VMEM((tokens, width), jnp.float32),
        ],
        compiler_params=pltpu.CompilerParams(vmem_limit_bytes=KERNEL_VMEM),
        name="out_spread",
    )(grads, powers, scale)


def square_scratch(width):
    return [
        pltpu.VMEM((BLOCK, BLOCK), jnp.float32),
        pltpu.VMEM((ITERS, BLOCK, BLOCK), jnp.bfloat16),
        pltpu.VMEM((BLOCK, width), jnp.float32),
    ]


def place_copies(places, refs, whole_ref, sem):
    core = lax.axis_index("dp") % 2
    chip = lax.axis_index("dp") // 2 % 2
    copies = []
    for (kind, first, second, *rest), ref in zip(places, refs):
        if kind == "full":
            block = 2 * second + (core if first else 1 - core)
            pieces, base, columns = PLACE_PARTS, 0, slice(None)
        else:
            block = whole_ref.shape[0] // BLOCK - 2 + (chip if first else 1 - chip)
            pieces, base = 1, rest[0]
            columns = aligned(core if second else 1 - core, ref.shape[1])
        span = ref.shape[0] // pieces
        for piece in range(pieces):
            rows = pl.ds(pl.multiple_of(block * BLOCK + base + piece * span, BLOCK // 8), span)
            copies.append(
                pltpu.make_async_copy(
                    ref.at[pl.ds(piece * span, span)],
                    whole_ref.at[rows, columns],
                    sem.at[len(copies)],
                )
            )
    return copies


def place_count(places):
    return max(1, sum(PLACE_PARTS if kind == "full" else 1 for kind, *_ in places))


def in_parts(count, parts, body):
    if parts == 1:
        for place in range(count):
            body(place)
        return
    inner = count // parts

    def turn(part, carry):
        for place in range(inner):
            body(part * inner + place)
        return carry

    lax.fori_loop(0, parts, turn, 0)


def right_side(pieces, spots, spread, prior, scale, wide, narrow, parts):
    span = pieces[0].shape[0]

    def tile(place):
        rows = aligned(place, TILE)
        value = prior[rows, :] if prior is not None else None
        for spot, piece in zip(spots, pieces):
            for part in spread:
                term = dot(piece[:, rows], part[spot * span : (spot + 1) * span, :], TN)
                value = term if value is None else value + term
        if scale is not None:
            value = value * scale
        wide[rows, :] = value
        if narrow is not None:
            narrow[rows, :] = value.astype(jnp.bfloat16)

    in_parts(BLOCK // TILE, parts, tile)


def apply_powers(powers, scale, wide, narrow):
    def apply(turn, carry):
        last = jnp.where(turn == ITERS - 1, scale, 1.0)
        for lo in range(0, wide.shape[1], TILE):
            cols = slice(lo, lo + TILE)
            value = 2.0 * wide[:, cols] - last * dot(
                powers[ITERS - 1 - turn], narrow[:, cols]
            )
            wide[:, cols] = value
            narrow[:, cols] = value.astype(jnp.bfloat16)
        return carry

    lax.fori_loop(0, ITERS, apply, 0)


def block_damping(damping_ref, block, blocks):
    return damping_ref[lax.axis_index("hid") * blocks + block]


def own_block(step):
    return 2 * step + lax.axis_index("dp") % 2


def block_kernel(begun, step, blocks, tokens, spots, places, held, damping_ref, *refs):
    parts = len(spots)
    pieces, spread, refs = refs[:parts], refs[parts : parts + 2], refs[parts + 2 :]
    prior, refs = (refs[0] if begun else None), refs[begun:]
    moving, refs = refs[: len(places)], refs[len(places) + held :]
    whole_ref, send_ref, factor, powers, wide, sem = refs
    copies = place_copies(places, moving, whole_ref, sem)
    start_all(copies)
    damping = block_damping(damping_ref, own_block(step), blocks)
    scale = scaled_factor(pieces[2 * begun :], prior, factor, powers, damping, tokens)
    residual_powers(factor, scale, powers)
    right_side(pieces, spots, spread, None, scale, wide, send_ref, 2)
    apply_powers(powers, scale, wide, send_ref)
    wait_all(copies)


def solo_kernel(begun, step, blocks, tokens, spots, places, held, damping_ref, *refs):
    parts = len(spots)
    pieces, spread, refs = refs[:parts], refs[parts : parts + 2], refs[parts + 2 :]
    prior, refs = (refs[0] if begun else None), refs[begun:]
    whole_ref, half_ref, *cut_refs = refs[:-4]
    factor, powers, wide, _ = refs[-4:]
    block = blocks - 2 + lax.axis_index("dp") // 2 % 2
    damping = block_damping(damping_ref, block, blocks)
    scale = scaled_factor(pieces[2 * begun :], prior, factor, powers, damping, tokens)
    residual_powers(factor, scale, powers)
    right_side(pieces, spots, spread, None, scale, wide, half_ref, 2)
    apply_powers(powers, scale, wide, half_ref)
    row = 0
    for cut_ref in cut_refs:
        cut_ref[...] = half_ref[row : row + cut_ref.shape[0], :]
        row += cut_ref.shape[0]


def early_kernel(step, blocks, tokens, spots, places, held, *refs):
    parts = len(spots)
    pieces, spread, refs = refs[:parts], refs[parts : parts + 2], refs[parts + 2 :]
    moving, refs = refs[: len(places)], refs[len(places) + held :]
    whole_ref, gram_ref, right_ref, sem = refs
    copies = place_copies(places, moving, whole_ref, sem)
    start_all(copies)
    upper_gram(pieces, gram_ref)
    right_side(pieces, spots, spread, None, None, right_ref, None, 2)
    wait_all(copies)


def late_kernel(step, blocks, tokens, spots, places, held, damping_ref, *refs):
    parts = len(spots)
    pieces, spread, refs = refs[:parts], refs[parts : parts + 2], refs[parts + 2 :]
    gram_ref, right_ref, refs = *refs[:2], refs[2:]
    moving, refs = refs[: len(places)], refs[len(places) + held :]
    whole_ref, send_ref, factor, powers, wide, sem = refs
    copies = place_copies(places, moving, whole_ref, sem)
    start_all(copies)
    damping = block_damping(damping_ref, own_block(step), blocks)
    scale = scaled_factor(pieces, gram_ref, factor, powers, damping, tokens)
    residual_powers(factor, scale, powers)
    right_side(pieces, spots, spread, right_ref, scale, wide, send_ref, 2)
    apply_powers(powers, scale, wide, send_ref)
    wait_all(copies)


def call(kernel, operands, specs, outs, out_specs, scratch_shapes, held):
    return pl.pallas_call(
        kernel,
        out_shape=outs,
        in_specs=specs,
        out_specs=out_specs,
        input_output_aliases={len(operands) - 1: 0} if held else {},
        scratch_shapes=scratch_shapes,
        compiler_params=pltpu.CompilerParams(vmem_limit_bytes=KERNEL_VMEM),
    )(*operands)


def block_call(kernel, name, step, blocks, tokens, damping, pieces, spread, extra, moving, whole):
    width = spread[0].shape[1]
    spots = sorted(pieces)
    held = whole is not None
    operands = [pieces[spot] for spot in spots] + [*spread, *extra, *moving.values()]
    specs = [VMEM] * len(operands)
    if damping is not None:
        operands, specs = [damping] + operands, [SMEM] + specs
    if held:
        operands, specs = operands + [whole], specs + [ANY]
    rows = blocks * BLOCK
    full = width * (2 if name == "solo" else 1)
    outs = [jax.ShapeDtypeStruct((rows, full), jnp.bfloat16)]
    if damping is None:
        outs.append(jax.ShapeDtypeStruct((BLOCK, BLOCK), jnp.float32))
        outs.append(jax.ShapeDtypeStruct((BLOCK, width), jnp.float32))
        shapes = []
    else:
        outs.append(jax.ShapeDtypeStruct((BLOCK, width), jnp.bfloat16))
        shapes = square_scratch(width)
    if name == "solo":
        outs += [jax.ShapeDtypeStruct((rows, width), jnp.bfloat16) for rows in SOLO_CUTS]
    places = list(moving)
    shapes = shapes + [pltpu.SemaphoreType.DMA((place_count(places),))]
    kernel = functools.partial(kernel, step, blocks, tokens, spots, places, held)
    out_specs = [ANY] + [VMEM] * (len(outs) - 1)
    return call(kernel, operands, specs, outs, out_specs, shapes, held)


def place_kernel(places, *refs):
    count = len(places)
    whole_ref, sem = refs[count + 1 :]
    copies = place_copies(places, refs[:count], whole_ref, sem)
    start_all(copies)
    wait_all(copies)


def place(moving, whole):
    places = list(moving)
    return call(
        functools.partial(place_kernel, places),
        [*moving.values(), whole],
        [VMEM] * len(places) + [ANY],
        jax.ShapeDtypeStruct(whole.shape, whole.dtype),
        ANY,
        [pltpu.SemaphoreType.DMA((place_count(places),))],
        True,
    )


def local(cuts, hidden_acts, out_grads, damping):
    span = hidden_acts.shape[0]
    tokens = span * lax.axis_size("dp")
    core = lax.axis_index("dp") % 2
    chip = lax.axis_index("dp") // 2 % 2
    blocks = hidden_acts.shape[1] // BLOCK
    steps = step_count(blocks)
    spots = range(1, lax.axis_size("dp"))

    small = span // cuts
    part = lax.dynamic_slice_in_dim(out_grads, lax.axis_index("hid") % cuts * small, small, 0)
    over = [swap(part, "dp", LATE)]
    over += [swap(over[0], "hid", cut) for cut in range(1, cuts)]
    side = swap(out_grads, "dp", 1)
    cross = [swap(over[cut], "dp", 1) for cut in range(cuts)]

    def columns(block):
        return lax.dynamic_slice_in_dim(hidden_acts, block * BLOCK, BLOCK, 1)

    if steps * 2 < blocks:
        mine, theirs = columns(blocks - 2 + chip), columns(blocks - 1 - chip)
        solo = {0: mine, 1: swap(mine, "dp", 1), 2: swap(theirs, "dp", 2)}
        solo[3] = swap(solo[2], "dp", 1)
    pieces = []
    for step in range(steps):
        same, other = columns(2 * step + core), columns(2 * step + 1 - core)
        pieces.append({0: same})
        for spot in spots:
            pieces[step][spot] = swap(other if spot % 2 else same, "dp", spot)

    begun = []
    if steps * 2 < blocks:
        begun = begin_grams([(out_grads, side), (solo[0], solo[1]), (pieces[0][0], pieces[0][1])])
    factor = out_factor_powers([out_grads, side, *over, *cross], begun[:1], cuts, tokens)
    high, low, high_half, low_half = precondition_grads(*factor)
    spread = (high, low)
    whole = None
    ready, final = {}, [{} for _ in range(2)]
    if steps * 2 < blocks:
        whole, half, *parts = block_call(
            functools.partial(solo_kernel, 1), "solo", None, blocks, tokens, damping, solo,
            (high_half, low_half), begun[1:2], {}, None,
        )
        ready["half", True, True, 0] = half
        upcoming = {("half", True, False, 0): swap(half, "dp", 1)}
        final += [{}, {}]
        row = 0
        for turn, part in enumerate(parts):
            got = swap(part, "dp", 2)
            passed = swap(got, "dp", 1)
            final[2 * turn]["half", False, True, row] = got
            final[turn + 2]["half", False, False, row] = passed
            row += part.shape[0]
    else:
        upcoming = {}
    for step in range(steps - 1):
        whole, send = block_call(
            functools.partial(block_kernel, len(begun[2:])), "block", step, blocks, tokens,
            damping, pieces[step], spread, begun[2:], ready, whole,
        )
        begun = []
        ready = {("full", True, step): send, **upcoming}
        upcoming = {("full", False, step): swap(send, "dp", 1)}
    step = steps - 1
    late = {LATE: pieces[step].pop(LATE)}
    whole, gram, right = block_call(
        early_kernel, "early", step, blocks, tokens, None, pieces[step], spread, (),
        ready, whole,
    )
    whole, send = block_call(
        late_kernel, "late", step, blocks, tokens, damping, late, spread, (gram, right),
        upcoming, whole,
    )
    final[0]["full", True, step] = send
    final[1]["full", False, step] = swap(send, "dp", 1)
    for moving in final:
        whole = place(moving, whole)
    return whole


def step_count(blocks):
    return (blocks - 2) // 2 if blocks > 4 else blocks // 2


def solution(mesh):
    hid_size = mesh.shape["hid"]
    cuts = min(GRAD_CUTS, hid_size & -hid_size)

    def body(hidden_acts, out_grads, damping):
        return local(cuts, hidden_acts, out_grads, damping)

    def run(hidden_acts, out_grads, damping):
        step = jax.shard_map(
            body,
            mesh=mesh,
            in_specs=(P("dp", "hid"), P("dp", None), P()),
            out_specs=P("hid", None),
            check_vma=False,
        )
        return step(hidden_acts, out_grads, damping)

    return run
```
